32 devices in a mesh: parts: 2 (over x), ctx: 16 (over z, y, core).
Axes of the slice: x: 2, y: 2, z: 4, core: 2. Of those that a mesh axis runs over, the one named last changes fastest.
Arguments:
- query_proj: bfloat16 [4096, 4096], P(('parts', 'ctx')), parts along dimension 0, may hold values from -6 to 6
- key_proj: bfloat16 [4096, 4096], P(('parts', 'ctx')), parts along dimension 0, may hold values from -6 to 6
- value_proj: bfloat16 [4096, 4096], P(('parts', 'ctx')), parts along dimension 0, may hold values from -6 to 6
- cotangent: bfloat16 [4096, 2048], P(('parts', 'ctx')), parts along dimension 0, may hold values from -6 to 6
- out_weight: bfloat16 [4096, 2048], P('ctx'), may hold values from -0.125 to 0.125
- filters: float32 [256, 2048], P('ctx'), may hold values from -1.2 to 1.2
Outputs:
- query_grad: float32 [4096, 4096], P(('parts', 'ctx')), parts along dimension 0
- key_grad: float32 [4096, 4096], P(('parts', 'ctx')), parts along dimension 0
- value_grad: float32 [4096, 4096], P(('parts', 'ctx')), parts along dimension 0
- filter_grad: float32 [512, 2048], P(('parts', 'ctx')), parts along dimension 0
The draws below stay inside these ranges and needn't reach their ends.
There are 2 independent parts, one for each index of `parts`. The reference program is written for one: setup_inputs(seed, part) draws one part's arguments, and reference() takes and returns one part's arrays. A program takes and returns all parts, laid end to end along the dimension named above; an argument that names none is the same for every part. Nothing has to cross between parts.
All inputs are finite; a program needn't handle non-finite values.
Results may differ from the reference program's by a relative error of at most 0.005.
Values may be sent and summed in bfloat16 or wider, within the bound.
No kernel may reach another device: no remote copies, remote signals or barrier semaphores. Data moves between devices by JAX's collectives and lax.ppermute only.
A program may use at most 192 MiB of HBM per device.

```python
import math
import jax
import jax.numpy as jnp
from jax import lax

D = 4096
DOUT = 2048
GROUP = 16
SEQ = 2048
GROUPS = 256


def draw_filters(key, part):
    key_tau, key_noise = jax.random.split(key)
    time_index = jnp.arange(SEQ, dtype=jnp.float32)[None, :]
    log_tau = jax.random.uniform(key_tau, (GROUPS, 1), jnp.float32, math.log(24.0), math.log(4.0 * SEQ))
    noise_field = jax.random.truncated_normal(key_noise, -4.0, 4.0, (GROUPS, SEQ), jnp.float32)
    decay_time = jnp.exp(log_tau)
    energy = 0.5 * decay_time * (1.0 - jnp.exp(-2.0 * SEQ / decay_time)) + 0.5
    return noise_field * jnp.exp(-time_index / decay_time) / jnp.sqrt(energy)


def steps_of(rng, dims, shards, low, high):
    loudness = 1.0
    for axis_at, shards_of in shards:
        steps = jax.random.uniform(jax.random.fold_in(jax.random.fold_in(rng, 6), axis_at), (shards_of,), jnp.float32, low / len(shards), high / len(shards))
        loudness = loudness * jnp.repeat(jnp.exp(steps), dims[axis_at] // shards_of).reshape((-1,) + (1,) * (len(dims) - 1 - axis_at))
    return loudness


def gaussian(key, dims, width, limit, pieces=(), kind=jnp.bfloat16):
    factor_of = steps_of(key, dims, pieces, -0.22, 0.18) if pieces else 1.0
    values = jax.random.normal(key, dims, jnp.float32) * width * factor_of
    return jnp.minimum(jnp.maximum(values, -limit), limit).astype(kind)


def setup_inputs(seed: int = 0, part: int = 0) -> dict:
    key_list = jax.random.split(jax.random.key(seed), 7)
    part_keys = jax.random.split(jax.random.fold_in(key_list[6], part), 7)
    query_proj = gaussian(part_keys[0], (SEQ, D), 1.0, 6.0, ((0, 16),))
    key_proj = gaussian(part_keys[1], (SEQ, D), 1.0, 6.0, ((0, 16),))
    value_proj = gaussian(part_keys[2], (SEQ, D), 1.0, 6.0, ((0, 16),))
    cotangent = gaussian(part_keys[3], (SEQ, DOUT), 1.0, 6.0, ((0, 16),))
    out_weight = gaussian(key_list[4], (D, DOUT), DOUT ** -0.5, 0.125, ((0, 16),))
    filters = draw_filters(jax.random.fold_in(key_list[6], 71), part)
    return {"query_proj": query_proj, "key_proj": key_proj, "value_proj": value_proj, "cotangent": cotangent, "out_weight": out_weight, "filters": filters}


def rounded_product(left, right):
    product = (left.astype(jnp.float32) * right.astype(jnp.float32)).astype(jnp.bfloat16)
    return lax.optimization_barrier(product).astype(jnp.float32)


def reference(query_proj, key_proj, value_proj, cotangent, out_weight, filters):
    grad_gated = jnp.dot(cotangent, out_weight.T, preferred_element_type=jnp.float32).astype(jnp.bfloat16)
    fft_len = 2 * SEQ
    grad_scale = (GROUP * SEQ) ** -0.5

    def regroup(array):
        return array.reshape(SEQ, GROUPS, GROUP).transpose(1, 0, 2)

    def one_group(inputs):
        query_block, key_block, value_block, grad_block, filter_row = inputs
        mixed = rounded_product(key_block, value_block)
        gated = rounded_product(query_block, grad_block)
        mixed_spec = jnp.fft.rfft(mixed, n=fft_len, axis=0)
        gated_spec = jnp.fft.rfft(gated, n=fft_len, axis=0)
        filter_spec = jnp.fft.rfft(filter_row, n=fft_len)[:, None]
        conv_out = jnp.fft.irfft(filter_spec * mixed_spec, n=fft_len, axis=0)[:SEQ]
        mixed_grad = jnp.fft.irfft(jnp.conj(filter_spec) * gated_spec, n=fft_len, axis=0)[:SEQ]
        lag_spec = jnp.sum(jnp.conj(mixed_spec) * gated_spec, axis=1)
        lag_sum = jnp.fft.irfft(lag_spec, n=fft_len)[:SEQ]
        query_part = grad_block.astype(jnp.float32) * conv_out
        key_part = mixed_grad * value_block.astype(jnp.float32)
        value_part = mixed_grad * key_block.astype(jnp.float32)
        return query_part, key_part, value_part, lag_sum * grad_scale

    query_all, key_all, value_all, filter_grad = lax.map(
        one_group, (regroup(query_proj), regroup(key_proj), regroup(value_proj), regroup(grad_gated), filters))

    def ungroup(array):
        return array.transpose(1, 0, 2).reshape(SEQ, D)

    return ungroup(query_all), ungroup(key_all), ungroup(value_all), filter_grad
```

```python
import math

import jax
import jax.numpy as jnp
from jax import lax
from jax.experimental import pallas as pl
from jax.experimental.pallas import tpu as pltpu
from jax.sharding import Mesh
from jax.sharding import PartitionSpec as P

inner_len = 128


def dft_pair(size_count):
    index_row = jnp.arange(size_count, dtype=jnp.int32)
    phase = (index_row[:, None] * index_row[None, :] % size_count).astype(jnp.float32) * (
        -2.0 * math.pi / size_count
    )
    return (jnp.cos(phase), jnp.sin(phase))


def twist(spectrum, sign):
    outer_len = spectrum.shape[1]
    total = outer_len * inner_len
    outer_index = jnp.arange(outer_len, dtype=jnp.int32)[:, None, None]
    inner_index = jnp.arange(inner_len, dtype=jnp.int32)[None, None, :]
    phase = (outer_index * inner_index % total).astype(jnp.float32) * (-2.0 * math.pi / total)
    tw_real = jnp.cos(phase)
    tw_imag = jnp.sin(phase) * sign
    real_part = spectrum[0] * tw_real - spectrum[1] * tw_imag
    imag_part = spectrum[0] * tw_imag + spectrum[1] * tw_real
    return jnp.stack([real_part, imag_part])


def last_matrix(sign):
    last_real, last_imag = dft_pair(inner_len)
    last_imag = last_imag * sign
    return jnp.stack([jnp.stack([last_real, -last_imag]), jnp.stack([last_imag, last_real])])


def apply_last(spectrum, sign):
    return jnp.einsum(
        "qzcn,pqkn->pzck", spectrum, last_matrix(sign), precision=lax.Precision.HIGHEST
    )


def forward_spectrum(signal):
    half_rows = signal.shape[0]
    outer_len = 2 * half_rows
    lead_real, lead_imag = dft_pair(outer_len)
    lead = jnp.stack([lead_real[:, :half_rows], lead_imag[:, :half_rows]])
    spectrum = jnp.einsum("pzn,ncm->pzcm", lead, signal, precision=lax.Precision.HIGHEST)
    return apply_last(twist(spectrum, 1.0), 1.0)


def inverse_spectrum(spectrum, want_imag):
    outer_len = spectrum.shape[1]
    half_rows = outer_len // 2
    spectrum = twist(apply_last(spectrum, -1.0), -1.0)
    lead_real, lead_imag = dft_pair(outer_len)
    lead_real = lead_real[:half_rows]
    lead_imag = lead_imag[:half_rows]
    scale = 1.0 / (outer_len * inner_len)
    if want_imag:
        lead = jnp.stack([jnp.stack([lead_real, lead_imag]), jnp.stack([-lead_imag, lead_real])])
    else:
        lead = jnp.stack([lead_real, lead_imag])[None]
    return jnp.einsum("qzcm,pqtz->ptcm", spectrum, lead * scale, precision=lax.Precision.HIGHEST)


def to_blocks(array):
    seq_len, chans = array.shape
    return (
        array.astype(jnp.float32).reshape(seq_len // inner_len, inner_len, chans).transpose(0, 2, 1)
    )


def from_blocks(array):
    half_rows, chans, unused = array.shape
    return array.transpose(0, 2, 1).reshape(half_rows * inner_len, chans)


def channel_work(mixed, gated, filters):
    seq_len, chans = mixed.shape
    group_count = filters.shape[0]
    group_size = chans // group_count
    half_rows = seq_len // inner_len
    outer_len = 2 * half_rows
    split_shape = (2, outer_len, group_count, group_size, inner_len)
    mix_spec = forward_spectrum(to_blocks(mixed)).reshape(split_shape)
    gate_spec = forward_spectrum(to_blocks(gated)).reshape(split_shape)
    filter_blocks = filters.reshape(group_count, half_rows, inner_len).transpose(1, 0, 2)
    filt_spec = forward_spectrum(filter_blocks)[:, :, :, None, :]
    filt_real, filt_imag = (filt_spec[0], filt_spec[1])
    mix_real, mix_imag = (mix_spec[0], mix_spec[1])
    gate_real, gate_imag = (gate_spec[0], gate_spec[1])
    conv_real = filt_real * mix_real - filt_imag * mix_imag
    conv_imag = filt_real * mix_imag + filt_imag * mix_real
    corr_real = filt_real * gate_real + filt_imag * gate_imag
    corr_imag = filt_real * gate_imag - filt_imag * gate_real
    combined = jnp.stack([conv_real - corr_imag, conv_imag + corr_real]).reshape(
        2, outer_len, chans, inner_len
    )
    both = inverse_spectrum(combined, True)
    conv_out = from_blocks(both[0])
    mixed_grad = from_blocks(both[1])
    lag_real = jnp.sum(mix_real * gate_real + mix_imag * gate_imag, axis=2)
    lag_imag = jnp.sum(mix_real * gate_imag - mix_imag * gate_real, axis=2)
    lag_out = inverse_spectrum(jnp.stack([lag_real, lag_imag]), False)[0]
    filter_grad = lag_out.transpose(1, 0, 2).reshape(group_count, seq_len) * (
        group_size * seq_len
    ) ** (-0.5)
    return (conv_out, mixed_grad, filter_grad)


def rounded_product(left, right):
    product = (left.astype(jnp.float32) * right.astype(jnp.float32)).astype(jnp.bfloat16)
    return lax.optimization_barrier(product)


def per_device_spectral(query_proj, key_proj, value_proj, cotangent, out_weight, filters):
    grad_rows = jnp.einsum(
        "tj,cj->tc",
        cotangent,
        lax.all_gather(out_weight, "ctx", axis=0, tiled=True),
        preferred_element_type=jnp.float32,
    ).astype(jnp.bfloat16)
    query_cols, key_cols, value_cols, grad_cols = (
        lax.all_to_all(query_proj, "ctx", split_axis=1, concat_axis=0, tiled=True),
        lax.all_to_all(key_proj, "ctx", split_axis=1, concat_axis=0, tiled=True),
        lax.all_to_all(value_proj, "ctx", split_axis=1, concat_axis=0, tiled=True),
        lax.all_to_all(grad_rows, "ctx", split_axis=1, concat_axis=0, tiled=True),
    )
    mixed_cols = rounded_product(key_cols, value_cols)
    gated_cols = rounded_product(query_cols, grad_cols)
    conv_out, mixed_grad, filter_grad = channel_work(mixed_cols, gated_cols, filters)
    query_grad_cols = grad_cols.astype(jnp.float32) * conv_out
    query_grad, key_grad, value_grad = (
        lax.all_to_all(query_grad_cols, "ctx", split_axis=0, concat_axis=1, tiled=True),
        lax.all_to_all(
            mixed_grad * value_cols.astype(jnp.float32),
            "ctx",
            split_axis=0,
            concat_axis=1,
            tiled=True,
        ),
        lax.all_to_all(
            mixed_grad * key_cols.astype(jnp.float32),
            "ctx",
            split_axis=0,
            concat_axis=1,
            tiled=True,
        ),
    )
    return (query_grad, key_grad, value_grad, filter_grad)


line_len = 4
quad_len = 4
lane = 128
group_width = 16


def nt_dot(left, right):
    return lax.dot_general(left, right, (((1,), (1,)), ((), ())), preferred_element_type=jnp.float32)


def split_kernel(*refs):
    count = (len(refs) - 1) // line_len - 1
    outs = refs[-line_len:]
    for step in range(line_len):
        block = refs[1 + count * step][...].astype(jnp.float32)
        if count == 2:
            block = block * refs[2 + count * step][...].astype(jnp.float32)
        outs[step][...] = block.T.astype(jnp.bfloat16)


def split_columns(place, *arrays):
    rows, chans = arrays[0].shape
    piece = chans // line_len
    cut = 2
    in_specs = []
    for step in range(line_len):
        for _ in arrays:
            in_specs.append(
                pl.BlockSpec(
                    (rows, piece // cut), lambda i, z, step=step: (0, (z[0] ^ step) * cut + i)
                )
            )
    return pl.pallas_call(
        split_kernel,
        grid_spec=pltpu.PrefetchScalarGridSpec(
            num_scalar_prefetch=1,
            grid=(cut,),
            in_specs=in_specs,
            out_specs=[pl.BlockSpec((piece // cut, rows), lambda i, z: (i, 0))] * line_len,
        ),
        out_shape=[jax.ShapeDtypeStruct((piece, rows), jnp.bfloat16)] * line_len,
        name="split_columns",
    )(place, *(list(arrays) * line_len))


def toeplitz_kernel(filter_ref, conv_ref, corr_ref):
    seq_len = filter_ref.shape[-1]
    wide = jnp.broadcast_to(filter_ref[0], (lane, seq_len))
    strip = pltpu.roll(wide, 0, 1, stride=1, stride_axis=0)
    row = lax.broadcasted_iota(jnp.int32, (lane, lane), 0)
    col = lax.broadcasted_iota(jnp.int32, (lane, lane), 1)
    for lag in range(seq_len // lane):
        tile = strip[:, lag * lane : (lag + 1) * lane]
        if lag == 0:
            tile = jnp.where(col >= row, tile, 0.0)
        rows = slice((lag % 2) * lane, (lag % 2 + 1) * lane)
        cols = slice((lag // 2) * lane, (lag // 2 + 1) * lane)
        conv_ref[0, rows, cols] = tile.astype(jnp.bfloat16)
        corr_ref[0, rows, cols] = tile.T.astype(jnp.bfloat16)


def toeplitz_tiles(filters):
    groups, seq_len = filters.shape
    shape = jax.ShapeDtypeStruct((groups, 2 * lane, seq_len // 2), jnp.bfloat16)
    spec = pl.BlockSpec((1, 2 * lane, seq_len // 2), lambda g: (g, 0, 0))
    return pl.pallas_call(
        toeplitz_kernel,
        grid=(groups,),
        in_specs=[pl.BlockSpec((1, 1, seq_len), lambda g: (g, 0, 0))],
        out_specs=[spec, spec],
        out_shape=[shape, shape],
        name="toeplitz_tiles",
    )(filters.reshape(groups, 1, seq_len))


def conv_kernel(place_ref, *refs):
    signals = refs[:line_len]
    tile_ref, out_ref = refs[line_len:]
    rows = line_len * quad_len * group_width
    signal = jnp.concatenate([s[...].reshape(quad_len * group_width, lane) for s in signals], axis=0)
    late = jnp.concatenate(
        [jnp.zeros((group_width, lane), signal.dtype), signal[: rows - group_width]], axis=0
    )
    both = jnp.concatenate([signal, late], axis=1)
    total = jnp.zeros((rows, lane), jnp.float32)
    for pair in range(0, line_len * quad_len // 2, 2):
        skip = 2 * group_width * pair
        part = jnp.dot(
            both[: rows - skip],
            tile_ref[0, :, pair * lane : (pair + 2) * lane],
            preferred_element_type=jnp.float32,
        )
        near = total[skip:] + part[:, :lane]
        shift = 2 * group_width
        near = jnp.concatenate(
            [near[:shift], near[shift:] + part[: rows - skip - shift, lane:]], axis=0
        )
        total = near if skip == 0 else jnp.concatenate([total[:skip], near], axis=0)
    result = total.astype(jnp.bfloat16).reshape(line_len, quad_len, group_width, lane)
    for z in range(line_len):
        out_ref[:, z] = result[z]


def convolve(place, mixed, tiles):
    chans = mixed.shape[2]
    groups = tiles.shape[0]
    specs = [
        pl.BlockSpec(
            (quad_len, None, group_width, lane), lambda g, p, z=z: (0, p[0] ^ z, g, 0)
        )
        for z in range(line_len)
    ]
    return pl.pallas_call(
        conv_kernel,
        grid_spec=pltpu.PrefetchScalarGridSpec(
            num_scalar_prefetch=1,
            grid=(groups,),
            in_specs=specs + [pl.BlockSpec((1,) + tiles.shape[1:], lambda g, p: (g, 0, 0))],
            out_specs=pl.BlockSpec(
                (quad_len, line_len, group_width, lane), lambda g, p: (0, 0, g, 0)
            ),
        ),
        out_shape=jax.ShapeDtypeStruct((quad_len, line_len, chans, lane), jnp.bfloat16),
        name="convolve",
    )(place, *([mixed] * line_len), tiles)


def corr_kernel(gated_ref, tile_ref, out_ref):
    rows = line_len * quad_len * group_width
    gated = jnp.concatenate(
        [gated_ref[:, z].reshape(quad_len * group_width, lane) for z in range(line_len)], axis=0
    )
    early = jnp.concatenate(
        [gated[group_width:], jnp.zeros((group_width, lane), gated.dtype)], axis=0
    )
    both = jnp.concatenate([gated, early], axis=1)
    total = jnp.zeros((rows, lane), jnp.float32)
    shift = 2 * group_width
    for pair in range(0, line_len * quad_len // 2, 2):
        skip = shift * pair
        part = jnp.dot(
            both[skip:],
            tile_ref[0, :, pair * lane : (pair + 2) * lane],
            preferred_element_type=jnp.float32,
        )
        near = total[: rows - skip] + part[:, :lane]
        near = jnp.concatenate(
            [near[: rows - skip - shift] + part[shift:, lane:], near[rows - skip - shift :]], axis=0
        )
        total = near if skip == 0 else jnp.concatenate([near, total[rows - skip :]], axis=0)
    result = total.astype(jnp.bfloat16).reshape(line_len, quad_len, group_width, lane)
    for z in range(line_len):
        out_ref[:, z] = result[z]


def correlate(gated, tiles):
    groups = tiles.shape[0]
    spec = pl.BlockSpec((quad_len, line_len, group_width, lane), lambda g: (0, 0, g, 0))
    return pl.pallas_call(
        corr_kernel,
        grid=(groups,),
        in_specs=[spec, pl.BlockSpec((1,) + tiles.shape[1:], lambda g: (g, 0, 0))],
        out_specs=spec,
        out_shape=jax.ShapeDtypeStruct(gated.shape, jnp.bfloat16),
        name="correlate",
    )(gated, tiles)


def lag_kernel(place_ref, *refs):
    signals = refs[:line_len]
    gated_ref, out_ref = refs[line_len:]
    rows = line_len * quad_len * group_width
    seq_len = line_len * quad_len * lane
    mixed = jnp.concatenate([s[...].reshape(quad_len * group_width, lane) for s in signals], axis=0)
    gated = jnp.concatenate(
        [gated_ref[:, z].reshape(quad_len * group_width, lane) for z in range(line_len)]
        + [jnp.zeros((rows, lane), gated_ref.dtype)],
        axis=0,
    )
    flipped = mixed.astype(jnp.float32).T.astype(jnp.bfloat16)
    parts = []
    for lag in range(0, line_len * quad_len, 2):
        first = gated[lag * group_width : lag * group_width + rows]
        second = gated[(lag + 1) * group_width : (lag + 1) * group_width + rows]
        parts.append(
            jnp.dot(
                flipped,
                jnp.concatenate([first, second], axis=1),
                preferred_element_type=jnp.float32,
            )
        )
    row = lax.broadcasted_iota(jnp.int32, (lane, 2 * lane), 0)
    col = lax.broadcasted_iota(jnp.int32, (lane, 2 * lane), 1)
    parts[0] = jnp.where(col >= row, parts[0], 0.0)
    total = jnp.concatenate(parts, axis=1)
    half = lane // 2
    while half >= 1:
        total = total[:half] + pltpu.roll(total[half:], seq_len - half, 1)
        half //= 2
    out_ref[0] = total * (group_width * seq_len) ** (-0.5)


def lag_sums(place, mixed, gated):
    groups = gated.shape[2] // group_width
    seq_len = line_len * quad_len * lane
    specs = [
        pl.BlockSpec(
            (quad_len, None, group_width, lane), lambda g, p, z=z: (0, p[0] ^ z, g, 0)
        )
        for z in range(line_len)
    ]
    sums = pl.pallas_call(
        lag_kernel,
        grid_spec=pltpu.PrefetchScalarGridSpec(
            num_scalar_prefetch=1,
            grid=(groups,),
            in_specs=specs
            + [pl.BlockSpec((quad_len, line_len, group_width, lane), lambda g, p: (0, 0, g, 0))],
            out_specs=pl.BlockSpec((1, 1, seq_len), lambda g, p: (g, 0, 0)),
        ),
        out_shape=jax.ShapeDtypeStruct((groups, 1, seq_len), jnp.float32),
        name="lag_sums",
    )(place, *([mixed] * line_len), gated)
    return sums.reshape(groups, seq_len)


def gate_kernel(place_ref, weight_ref, *refs):
    cots = refs[:line_len]
    queries = refs[line_len : 2 * line_len]
    grad_ref, gated_ref = refs[2 * line_len :]
    for step in range(line_len):
        at = place_ref[0] ^ step
        grad = nt_dot(weight_ref[...], cots[step][...]).astype(jnp.bfloat16)
        grad_ref[0, at] = grad
        query = queries[step][...].astype(jnp.float32)
        gated_ref[0, at] = (query * grad.astype(jnp.float32)).astype(jnp.bfloat16)


def gate(place, weights, cots, queries):
    chans = weights.shape[0] // quad_len
    feats = weights.shape[1]
    near = line_len - 1
    cot_specs = [
        pl.BlockSpec(
            (None, lane, feats), lambda i, z, k=k: (near + (z[0] ^ k) - z[0], 0, 0)
        )
        for k in range(line_len)
    ]
    spec = pl.BlockSpec((1, line_len, chans, lane), lambda i, z: (i, 0, 0, 0))
    shape = jax.ShapeDtypeStruct((quad_len, line_len, chans, lane), jnp.bfloat16)
    return pl.pallas_call(
        gate_kernel,
        grid_spec=pltpu.PrefetchScalarGridSpec(
            num_scalar_prefetch=1,
            grid=(quad_len,),
            in_specs=[pl.BlockSpec((chans, feats), lambda i, z: (i, 0))]
            + cot_specs
            + [pl.BlockSpec((chans, lane), lambda i, z: (i, 0))] * line_len,
            out_specs=[spec, spec],
        ),
        out_shape=[shape, shape],
        name="gate",
    )(place, weights, *([cots] * line_len), *queries)


def query_kernel(place_ref, grad_ref, conv_ref, *outs):
    for step in range(line_len):
        at = place_ref[0] ^ step
        product = grad_ref[0, at].astype(jnp.float32) * conv_ref[0, at].astype(jnp.float32)
        outs[step][...] = product.astype(jnp.bfloat16)


def query_pieces(place, grad, conv):
    chans = grad.shape[2]
    spec = pl.BlockSpec((1, line_len, chans, lane), lambda i, z: (i, 0, 0, 0))
    return pl.pallas_call(
        query_kernel,
        grid_spec=pltpu.PrefetchScalarGridSpec(
            num_scalar_prefetch=1,
            grid=(quad_len,),
            in_specs=[spec, spec],
            out_specs=[pl.BlockSpec((chans, lane), lambda i, z: (i, 0))] * line_len,
        ),
        out_shape=[jax.ShapeDtypeStruct((quad_len * chans, lane), jnp.bfloat16)] * line_len,
        name="query_pieces",
    )(place, grad, conv)


def pieces_kernel(place_ref, conv_ref, *outs):
    for step in range(line_len):
        outs[step][...] = conv_ref[0, place_ref[0] ^ step]


def line_pieces(place, array):
    chans = array.shape[2]
    spec = pl.BlockSpec((1, line_len, chans, lane), lambda i, z: (i, 0, 0, 0))
    return pl.pallas_call(
        pieces_kernel,
        grid_spec=pltpu.PrefetchScalarGridSpec(
            num_scalar_prefetch=1,
            grid=(quad_len,),
            in_specs=[spec],
            out_specs=[pl.BlockSpec((chans, lane), lambda i, z: (i, 0))] * line_len,
        ),
        out_shape=[jax.ShapeDtypeStruct((quad_len * chans, lane), jnp.bfloat16)] * line_len,
        name="line_pieces",
    )(place, array)


def merge_columns(place, pieces, factors):
    piece, rows = pieces[0].shape
    spec = pl.BlockSpec((rows, piece), lambda i, z: (0, i))
    outs = max(1, len(factors))

    def kernel(place_ref, *refs):
        parts = refs[:line_len]
        factor_refs = refs[line_len : line_len + len(factors)]
        out_refs = refs[line_len + len(factors) :]
        for step in range(line_len):

            @pl.when((pl.program_id(0) ^ place_ref[0]) == step)
            def _():
                block = parts[step][...].astype(jnp.float32).T
                if factor_refs:
                    for factor, out in zip(factor_refs, out_refs):
                        out[...] = block * factor[...].astype(jnp.float32)
                else:
                    out_refs[0][...] = block

    return pl.pallas_call(
        kernel,
        grid_spec=pltpu.PrefetchScalarGridSpec(
            num_scalar_prefetch=1,
            grid=(line_len,),
            in_specs=[pl.BlockSpec((piece, rows), lambda i, z: (0, 0))] * line_len
            + [spec] * len(factors),
            out_specs=[spec] * outs,
        ),
        out_shape=[jax.ShapeDtypeStruct((rows, piece * line_len), jnp.float32)] * outs,
        name="merge_columns",
    )(place, *pieces, *factors)


def line_exchange(pieces):
    return [pieces[0]] + [
        lax.ppermute(pieces[step], "line", [(i, i ^ step) for i in range(line_len)])
        for step in range(1, line_len)
    ]


def line_gather(array):
    right = [(i, i + 1) for i in range(line_len - 1)]
    left = [(i + 1, i) for i in range(line_len - 1)]
    lower, upper = ([], [])
    from_lower = from_upper = array
    for _ in range(line_len - 1):
        from_lower = lax.ppermute(from_lower, "line", right)
        from_upper = lax.ppermute(from_upper, "line", left)
        lower.append(from_lower)
        upper.append(from_upper)
    return jnp.stack(lower[::-1] + [array] + upper)


def quad_gather(array):
    across = lax.ppermute(array, "quad", [(i, i ^ 2) for i in range(quad_len)])
    row = lax.axis_index("quad") // 2
    pair = jnp.where(row == 0, jnp.stack([array, across]), jnp.stack([across, array]))
    other = lax.ppermute(pair, "quad", [(i, i ^ 1) for i in range(quad_len)])
    core = lax.axis_index("quad") % 2
    both = jnp.where(core == 0, jnp.stack([pair, other], 1), jnp.stack([other, pair], 1))
    return both.reshape(quad_len * array.shape[0], array.shape[1])


def quad_exchange(array):
    return lax.all_to_all(array, "quad", split_axis=0, concat_axis=0, tiled=True)


def per_device_line(query_proj, key_proj, value_proj, cotangent, out_weight, filters):
    place = lax.axis_index("line").reshape(1).astype(jnp.int32)
    chans = out_weight.shape[0]
    cots = line_gather(cotangent)
    weights = quad_gather(out_weight)
    mixed_pieces = line_exchange(split_columns(place, key_proj, value_proj))
    query_parts = line_exchange(split_columns(place, query_proj))
    conv_tiles, corr_tiles = toeplitz_tiles(filters)
    mixed = jnp.concatenate(
        [piece.reshape(quad_len, 1, chans, lane) for piece in mixed_pieces], axis=1
    )
    mixed = quad_exchange(mixed)
    conv = quad_exchange(convolve(place, mixed, conv_tiles))
    grad, gated = gate(place, weights, cots, query_parts)
    gated = quad_exchange(gated)
    query_back = line_exchange(query_pieces(place, grad, conv))
    mixed_grad = quad_exchange(correlate(gated, corr_tiles))
    mixed_back = line_exchange(line_pieces(place, mixed_grad))
    filter_grad = lag_sums(place, mixed, gated)
    (query_grad,) = merge_columns(place, query_back, ())
    key_grad, value_grad = merge_columns(place, mixed_back, (value_proj, key_proj))
    return (query_grad, key_grad, value_grad, filter_grad)


def solution(mesh):
    rows = P(("parts", "ctx"), None)
    shared = P("ctx", None)
    body = per_device_spectral
    if mesh.shape["ctx"] == line_len * quad_len:
        parts = mesh.shape["parts"]
        mesh = Mesh(
            mesh.devices.reshape(parts, line_len, quad_len), ("parts", "line", "quad")
        )
        rows = P(("parts", "line", "quad"), None)
        shared = P(("line", "quad"), None)
        body = per_device_line
    return jax.shard_map(
        body,
        mesh=mesh,
        in_specs=(rows, rows, rows, rows, shared, shared),
        out_specs=(rows, rows, rows, rows),
        check_vma=False,
    )
```
